32 devices in a mesh: groups: 2 (over y), ctx: 8 (over z, core), tp: 2 (over x), section: 1.
Axes of the slice: x: 2, y: 2, z: 4, core: 2. Of those that a mesh axis runs over, the one named last changes fastest.
Arguments:
- doc_lengths: int32 [8], P('groups'), parts along dimension 0, may hold values from 1 to 1024, 2048 in all
- queries: bfloat16 [1, 4096, 2048], P('section', ('groups', 'ctx'), 'tp'), parts along dimension 1, may hold values from -30 to 30
- keys: bfloat16 [1, 4096, 1024], P('section', ('groups', 'ctx'), 'tp'), parts along dimension 1, may hold values from -30 to 30
- values: bfloat16 [1, 4096, 1024], P('section', ('groups', 'ctx'), 'tp'), parts along dimension 1, may hold values from -6 to 6
- out_grad: bfloat16 [1, 4096, 2048], P('section', ('groups', 'ctx'), 'tp'), parts along dimension 1, may hold values from -6 to 6
Outputs:
- attn_out: bfloat16 [1, 4096, 2048], P('section', ('groups', 'ctx'), 'tp'), parts along dimension 1
- grad_queries: bfloat16 [1, 4096, 2048], P('section', ('groups', 'ctx'), 'tp'), parts along dimension 1
- grad_keys: bfloat16 [1, 4096, 1024], P('section', ('groups', 'ctx'), 'tp'), parts along dimension 1
- grad_values: bfloat16 [1, 4096, 1024], P('section', ('groups', 'ctx'), 'tp'), parts along dimension 1
The draws below stay inside these ranges and needn't reach their ends.
There are 2 independent parts, one for each index of `groups`. The reference program is written for one: setup_inputs(seed, part) draws one part's arguments, and reference() takes and returns one part's arrays. A program takes and returns all parts, laid end to end along the dimension named above; each array names one. Nothing has to cross between parts.
All inputs are finite; a program needn't handle non-finite values.
Results may differ from the reference program's by a relative error of at most 0.02.
Values may be sent and summed in bfloat16 or wider, within the bound.
A program may use at most 64 MiB of HBM per device.

```python
import math
import jax
import jax.numpy as jnp
import numpy as np
from jax import lax

HEAD_DIM = 256
HEADS = 8
KV_HEADS = 4
LOOKBACK_SIZE = 2048
TOKENS = 2048
LAYERS = 1
DOCS = 4
MOSTDOC = 1024


def draw_queries(key, part):
    group = HEADS // KV_HEADS
    rough = jax.random.truncated_normal(jax.random.fold_in(key, 1), -5.0, 5.0, (LAYERS, TOKENS, KV_HEADS, group, HEAD_DIM), jnp.float32)
    return rough.reshape(LAYERS, TOKENS, HEADS * HEAD_DIM).astype(jnp.bfloat16)


def draw_keys(key, part):
    rough = jax.random.truncated_normal(jax.random.fold_in(key, 3), -5.0, 5.0, (LAYERS, TOKENS, KV_HEADS, HEAD_DIM), jnp.float32)
    return rough.reshape(LAYERS, TOKENS, KV_HEADS * HEAD_DIM).astype(jnp.bfloat16)


def steps_of(key, dims, pieces, low, high):
    level, own = 1.0, jax.random.fold_in(key, 6)
    for axis_at, blocks in pieces:
        heights = jnp.exp(jax.random.uniform(jax.random.fold_in(own, axis_at), (blocks,), jnp.float32, low / len(pieces), high / len(pieces)))
        level = level * jnp.repeat(heights, dims[axis_at] // blocks).reshape([-1 if axis == axis_at else 1 for axis in range(len(dims))])
    return level


def split_up(number_of, total, limit, skew):
    loads = [(1 << 20) // math.isqrt(standing ** skew) + 1 for standing in range(2, number_of + 1)]
    surplus, counts = total - limit - (number_of - 1), [1] * (number_of - 1)
    while surplus > 0:
        free = [i for i in range(number_of - 1) if counts[i] < limit]
        whole, budget = sum([loads[i] for i in free]), surplus
        for i in free:
            more = min(limit - counts[i], max(1, budget * loads[i] // whole), surplus)
            counts[i] = counts[i] + more
            surplus = surplus - more
    return np.array([limit] + counts)


def ragged_sizes(stream_key, amount, total, most, lean):
    if amount == 2:
        one = jax.random.randint(stream_key, (), max(1, total - most), min(most, total - 1) + 1)
        return jnp.stack([one, total - one])
    sizes = jnp.asarray(split_up(amount, total, most, lean), jnp.int32)
    pairs = (amount - 1) // 2
    source_of, sink = sizes[1:1 + 2 * pairs:2], sizes[2:2 + 2 * pairs:2]
    margin = jnp.minimum(source_of - 1, most - sink)
    shifted = jax.random.randint(jax.random.fold_in(stream_key, 1), (pairs,), 0, 1 << 20) % (margin + 1)
    sizes = sizes.at[1:1 + 2 * pairs:2].set(source_of - shifted).at[2:2 + 2 * pairs:2].set(sink + shifted)
    return sizes[jax.random.permutation(jax.random.fold_in(stream_key, 2), amount)]


def gaussian(rng, shape, scale, reach, shards=(), held_as=jnp.bfloat16):
    result = scale * jax.random.normal(rng, shape, jnp.float32)
    if shards:
        result = result * steps_of(rng, shape, shards, -0.22, 0.18)
    return jnp.clip(result, -reach, reach).astype(held_as)


def setup_inputs(seed: int = 0, part: int = 0) -> dict:
    arg_keys = jax.random.split(jax.random.key(seed), 6)
    part_splits = jax.random.split(jax.random.fold_in(arg_keys[5], part), 6)
    doc_lengths = ragged_sizes(part_splits[0], DOCS, TOKENS, MOSTDOC, 2).astype(jnp.int32)
    queries = draw_queries(jax.random.fold_in(jax.random.fold_in(arg_keys[5], part), 71), part)
    keys = draw_keys(jax.random.fold_in(jax.random.fold_in(arg_keys[5], part), 71), part)
    values = gaussian(part_splits[3], (LAYERS, TOKENS, KV_HEADS * HEAD_DIM), 1.0, 6.0, ((1, 8), (2, 2)))
    out_grad = gaussian(part_splits[4], (LAYERS, TOKENS, HEADS * HEAD_DIM), 1.0, 6.0, ((1, 8), (2, 2)))
    return {"doc_lengths": doc_lengths, "queries": queries, "keys": keys, "values": values, "out_grad": out_grad}


def layer_pass(offsets, q_all, k_all, value_rows_full, g_all):
    block = math.gcd(TOKENS, 512)
    group = HEADS // KV_HEADS
    scale = HEAD_DIM ** -0.5
    key_window_width = KV_HEADS * HEAD_DIM
    window_extent = LOOKBACK_SIZE + block
    kpad = jnp.concatenate([jnp.zeros((LOOKBACK_SIZE, key_window_width), k_all.dtype), k_all], axis=0)
    value_padded = jnp.concatenate([jnp.zeros((LOOKBACK_SIZE, key_window_width), value_rows_full.dtype), value_rows_full], axis=0)
    zero_acc = jnp.zeros((TOKENS + LOOKBACK_SIZE, key_window_width), jnp.float32)

    def step(carry, index):
        dk_acc, dv_acc = carry
        leading_position = (index * block).astype(jnp.int32)
        qb = lax.dynamic_slice_in_dim(q_all, leading_position, block, 0).astype(jnp.float32)
        gb = lax.dynamic_slice_in_dim(g_all, leading_position, block, 0).astype(jnp.float32)
        kb = lax.dynamic_slice_in_dim(kpad, leading_position, window_extent, 0).astype(jnp.float32)
        value_block = lax.dynamic_slice_in_dim(value_padded, leading_position, window_extent, 0).astype(jnp.float32)
        qpos = leading_position + jnp.arange(block, dtype=jnp.int32)
        kpos = leading_position - LOOKBACK_SIZE + jnp.arange(window_extent, dtype=jnp.int32)
        starts = jnp.max(jnp.where(offsets[None, :] <= qpos[:, None], offsets[None, :], 0), axis=1)
        allowed = (kpos[None, :] <= qpos[:, None]) & (kpos[None, :] > qpos[:, None] - LOOKBACK_SIZE) & (kpos[None, :] >= starts[:, None])
        qh = qb.reshape(block, KV_HEADS, group, HEAD_DIM)
        gh = gb.reshape(block, KV_HEADS, group, HEAD_DIM)
        kh = kb.reshape(window_extent, KV_HEADS, HEAD_DIM)
        vh = value_block.reshape(window_extent, KV_HEADS, HEAD_DIM)
        scores = jnp.einsum("igpd,jgd->gpij", qh, kh) * scale
        masked = jnp.where(allowed[None, None], scores, -1e30)
        top = jnp.max(masked, axis=-1, keepdims=True)
        expo = jnp.exp(masked - top)
        prob = expo / jnp.sum(expo, axis=-1, keepdims=True)
        prob_low = lax.optimization_barrier(prob.astype(jnp.bfloat16)).astype(jnp.float32)
        outh = jnp.einsum("gpij,jgd->igpd", prob_low, vh)
        attn_low = outh.astype(jnp.bfloat16)
        attn_back = lax.optimization_barrier(attn_low).astype(jnp.float32)
        delta = jnp.moveaxis(jnp.sum(gh * attn_back, axis=-1), 0, -1)
        dprob = jnp.einsum("igpd,jgd->gpij", gh, vh)
        dscore = (prob * (dprob - delta[..., None]) * scale).astype(jnp.bfloat16)
        dscore = lax.optimization_barrier(dscore).astype(jnp.float32)
        dq = jnp.einsum("gpij,jgd->igpd", dscore, kh).astype(jnp.bfloat16)
        dk_part = jnp.einsum("gpij,igpd->jgd", dscore, qh).reshape(window_extent, key_window_width)
        dv_part = jnp.einsum("gpij,igpd->jgd", prob_low, gh).reshape(window_extent, key_window_width)
        dk_acc = lax.dynamic_update_slice_in_dim(dk_acc, lax.dynamic_slice_in_dim(dk_acc, leading_position, window_extent, 0) + dk_part, leading_position, 0)
        dv_acc = lax.dynamic_update_slice_in_dim(dv_acc, lax.dynamic_slice_in_dim(dv_acc, leading_position, window_extent, 0) + dv_part, leading_position, 0)
        return (dk_acc, dv_acc), (attn_low.reshape(block, HEADS * HEAD_DIM), dq.reshape(block, HEADS * HEAD_DIM))

    count = TOKENS // block
    (dk_acc, dv_acc), (attn_blocks, dq_blocks) = lax.scan(step, (zero_acc, zero_acc), jnp.arange(count, dtype=jnp.int32))
    attn = attn_blocks.reshape(TOKENS, HEADS * HEAD_DIM)
    dq_all = dq_blocks.reshape(TOKENS, HEADS * HEAD_DIM)
    return attn, dq_all, dk_acc[LOOKBACK_SIZE:].astype(jnp.bfloat16), dv_acc[LOOKBACK_SIZE:].astype(jnp.bfloat16)


def reference(doc_lengths, queries, keys, values, out_grad):
    offsets = (jnp.cumsum(doc_lengths) - doc_lengths).astype(jnp.int32)
    results = [layer_pass(offsets, queries[layer], keys[layer], values[layer], out_grad[layer]) for layer in range(LAYERS)]
    attn_out = jnp.stack([item[0] for item in results])
    grad_queries = jnp.stack([item[1] for item in results])
    grad_keys = jnp.stack([item[2] for item in results])
    grad_values = jnp.stack([item[3] for item in results])
    return (attn_out, grad_queries, grad_keys, grad_values)
```

```python
import jax
import jax.numpy as jnp
from jax import lax
from jax.sharding import PartitionSpec as P

HEAD_DIM = 256
LOOKBACK_SIZE = 2048


def passed_along(block, axis, distance):
    devices = range(lax.axis_size(axis))
    route = [(i - distance, i) for i in devices if i - distance in devices]
    return lax.ppermute(block, axis, route)


def body(doc_lengths, queries, keys, values, out_grad):
    q_here = queries[0]
    k_here = keys[0]
    v_here = values[0]
    g_here = out_grad[0]
    tok = q_here.shape[0]
    key_window_width = k_here.shape[1]
    kv_here = key_window_width // HEAD_DIM
    group = q_here.shape[1] // key_window_width
    longest = tok * lax.axis_size("ctx") // 2
    reach = -(-min(LOOKBACK_SIZE, longest) // tok)
    scale = HEAD_DIM ** (-0.5)
    shard = lax.axis_index("ctx")
    tiles_k = [k_here]
    tiles_v = [v_here]
    for step in range(1, reach + 1):
        got_k, got_v = passed_along((k_here, v_here), "ctx", step)
        tiles_k.insert(0, got_k)
        tiles_v.insert(0, got_v)
    win_k = jnp.concatenate(tiles_k, axis=0)
    win_v = jnp.concatenate(tiles_v, axis=0)
    window_extent = win_k.shape[0]
    offsets = jnp.cumsum(doc_lengths) - doc_lengths
    qpos = shard * tok + jnp.arange(tok, dtype=jnp.int32)
    kpos = (shard - reach) * tok + jnp.arange(window_extent, dtype=jnp.int32)
    starts = jnp.max(jnp.where(offsets[None, :] <= qpos[:, None], offsets[None, :], 0), axis=1)
    allowed = (
        (kpos[None, :] <= qpos[:, None])
        & (kpos[None, :] > qpos[:, None] - LOOKBACK_SIZE)
        & (kpos[None, :] >= starts[:, None])
    )
    qh = q_here.reshape(tok, kv_here, group, HEAD_DIM)
    gh = g_here.reshape(tok, kv_here, group, HEAD_DIM)
    kh = win_k.reshape(window_extent, kv_here, HEAD_DIM)
    vh = win_v.reshape(window_extent, kv_here, HEAD_DIM)
    scores = jnp.einsum("igpd,jgd->gpij", qh, kh, preferred_element_type=jnp.float32) * scale
    masked = jnp.where(allowed[None, None], scores, -1e30)
    top = jnp.max(masked, axis=-1, keepdims=True)
    expo = jnp.exp(masked - top)
    prob = expo / jnp.sum(expo, axis=-1, keepdims=True)
    prob_low = prob.astype(jnp.bfloat16)
    outh = jnp.einsum("gpij,jgd->igpd", prob_low, vh, preferred_element_type=jnp.float32)
    attn_low = outh.astype(jnp.bfloat16)
    attn_back = lax.optimization_barrier(attn_low).astype(jnp.float32)
    delta = jnp.moveaxis(jnp.sum(gh.astype(jnp.float32) * attn_back, axis=-1), 0, -1)
    dprob = jnp.einsum("igpd,jgd->gpij", gh, vh, preferred_element_type=jnp.float32)
    dscore = (prob * (dprob - delta[..., None]) * scale).astype(jnp.bfloat16)
    grad_q = jnp.einsum("gpij,jgd->igpd", dscore, kh, preferred_element_type=jnp.float32).astype(
        jnp.bfloat16
    )
    part_k = jnp.einsum("gpij,igpd->jgd", dscore, qh, preferred_element_type=jnp.float32).reshape(
        window_extent, key_window_width
    )
    part_v = jnp.einsum("gpij,igpd->jgd", prob_low, gh, preferred_element_type=jnp.float32).reshape(
        window_extent, key_window_width
    )
    own_k = part_k[reach * tok :]
    own_v = part_v[reach * tok :]
    for step in range(1, reach + 1):
        low = (reach - step) * tok
        back_k, back_v = (
            passed_along(part_k[low : low + tok].astype(jnp.bfloat16), "ctx", -step).astype(
                jnp.float32
            ),
            passed_along(part_v[low : low + tok].astype(jnp.bfloat16), "ctx", -step).astype(
                jnp.float32
            ),
        )
        own_k = own_k + back_k
        own_v = own_v + back_v
    attn_flat = attn_low.reshape(tok, kv_here * group * HEAD_DIM)
    grad_flat = grad_q.reshape(tok, kv_here * group * HEAD_DIM)
    return (
        attn_flat[None],
        grad_flat[None],
        own_k.astype(jnp.bfloat16)[None],
        own_v.astype(jnp.bfloat16)[None],
    )


def solution(mesh):
    placed = (
        P("groups"),
        P("section", ("groups", "ctx"), "tp"),
        P("section", ("groups", "ctx"), "tp"),
        P("section", ("groups", "ctx"), "tp"),
        P("section", ("groups", "ctx"), "tp"),
    )
    return jax.shard_map(
        body,
        mesh=mesh,
        in_specs=placed,
        out_specs=(
            P("section", ("groups", "ctx"), "tp"),
            P("section", ("groups", "ctx"), "tp"),
            P("section", ("groups", "ctx"), "tp"),
            P("section", ("groups", "ctx"), "tp"),
        ),
        check_vma=False,
    )
```

```python
import functools

import jax
import jax.numpy as jnp
from jax import lax
from jax.experimental import pallas as pl
from jax.experimental.pallas import tpu as pltpu
from jax.sharding import PartitionSpec as P

HEAD_DIM = 256
LOOKBACK_SIZE = 2048
F32 = jnp.float32
BF16 = jnp.bfloat16
CONTRACT_LAST = (((1,), (1,)), ((), ()))
CONTRACT_FIRST = (((0,), (0,)), ((), ()))


def kernel(
    n, hops, docs_ref, q_ref, k_ref, v_ref, g_ref, o_ref, dq_ref, dk_ref, dv_ref,
    win, q2, g2, s_ref, p_ref, dp_ref, acc, sbuf, cbuf, rsib, rchain,
    fs, fr, ss, sr, bs, br, cs, cr,
):
    tok = q_ref.shape[0]
    kv = k_ref.shape[1] // HEAD_DIM
    group = q_ref.shape[1] // k_ref.shape[1]
    cols = group * tok
    slots = 2 * hops + 1
    scale = HEAD_DIM ** (-0.5)
    d = lax.axis_index("ctx")
    c = lax.rem(d, 2)
    up = lax.rem(d + 2, n)
    down = lax.rem(d + n - 2, n)
    sibling = d + 1 - 2 * c

    def remote(src, dst, send, recv, device):
        return pltpu.make_async_remote_copy(
            src_ref=src, dst_ref=dst, send_sem=send, recv_sem=recv,
            device_id={"ctx": device}, device_id_type=pl.DeviceIdType.MESH,
        )

    def fwd(x, t):
        return remote(win.at[x, 2 * t - 2], win.at[x, 2 * t], fs.at[x, t - 1], fr.at[x, t - 1], up)

    def sib(x, u):
        return remote(win.at[x, 2 * u + 2 * c], win.at[x, 2 * u + 1], ss.at[x, u], sr.at[x, u], sibling)

    def bsib(x, u):
        return remote(sbuf.at[x, u], rsib.at[x, u], bs.at[x, u], br.at[x, u], sibling)

    def chain(x, t):
        return remote(cbuf.at[x, t - 1], rchain.at[x, t - 1], cs.at[x, t - 1], cr.at[x, t - 1], down)

    def start_own(x):
        @pl.when(d + 2 < n)
        def _():
            fwd(x, 1).start()

        @pl.when(c == 0)
        def _():
            sib(x, 0).start()

    def arrive(x, t):
        @pl.when(d >= 2 * t)
        def _():
            fwd(x, t).wait_recv()
            if t < hops:
                @pl.when(d + 2 < n)
                def _():
                    fwd(x, t + 1).start()

                @pl.when(c == 0)
                def _():
                    sib(x, t).start()

            @pl.when(c == 1)
            def _():
                sib(x, t - 1).start()

    def arrive_sib(x):
        for u in range(hops):
            @pl.when(d >= 2 * u + 1)
            def _():
                sib(x, u).wait_recv()

    def send_odd(x, u, part):
        sbuf[x, u] = part.astype(BF16)

        @pl.when(d >= 2 * u + 1)
        def _():
            bsib(x, u).start()

    def chain_step(x, t, out_ref, lo):
        @pl.when(d >= 2 * t)
        def _():
            if t < hops:
                @pl.when(c == 0)
                def _():
                    bsib(x, t).wait_recv()
                    acc[x, t] += rsib[x, t].astype(F32)
            if t >= 1:
                @pl.when(c == 1)
                def _():
                    bsib(x, t - 1).wait_recv()
                    acc[x, t] += rsib[x, t - 1].astype(F32)
            if t < hops:
                @pl.when(d + 2 < n)
                def _():
                    chain(x, t + 1).wait_recv()
                    acc[x, t] += rchain[x, t].astype(F32)
            if t > 0:
                cbuf[x, t - 1] = acc[x, t].astype(BF16)
                chain(x, t).start()
            else:
                out_ref[:, lo : lo + HEAD_DIM] = acc[x, t].astype(BF16)

    def finish_sends(x):
        for t in range(1, hops + 1):
            @pl.when((d + 2 < n) & (d >= 2 * t - 2))
            def _():
                fwd(x, t).wait_send()

            @pl.when(d >= 2 * t)
            def _():
                chain(x, t).wait_send()
        for u in range(hops):
            @pl.when(d >= 2 * u + 2 * c)
            def _():
                sib(x, u).wait_send()

            @pl.when(d >= 2 * u + 1)
            def _():
                bsib(x, u).wait_send()

    barrier = pltpu.get_barrier_semaphore()
    for other in (up, down, sibling):
        pl.semaphore_signal(
            barrier, inc=1, device_id={"ctx": other}, device_id_type=pl.DeviceIdType.MESH
        )
    for h in range(kv):
        lo = h * HEAD_DIM
        win[2 * h, 0] = k_ref[:, lo : lo + HEAD_DIM]
        win[2 * h + 1, 0] = v_ref[:, lo : lo + HEAD_DIM]
    pl.semaphore_wait(barrier, 3)
    start_own(0)
    start_own(1)

    for r in range(1, slots):
        @pl.when(d < r)
        def _():
            for x in range(2 * kv):
                win[x, r] = jnp.zeros((tok, HEAD_DIM), BF16)
    for h in range(kv):
        for e in range(group):
            lo = (h * group + e) * HEAD_DIM
            q2[h, e * tok : (e + 1) * tok, :] = q_ref[:, lo : lo + HEAD_DIM]
            g2[h, e * tok : (e + 1) * tok, :] = g_ref[:, lo : lo + HEAD_DIM]

    qpos = d * tok + lax.rem(lax.broadcasted_iota(jnp.int32, (1, cols), 1), tok)
    low = jnp.zeros((1, cols), jnp.int32)
    offset = jnp.int32(0)
    for i in range(docs_ref.shape[0]):
        low = jnp.where(offset <= qpos, jnp.maximum(low, offset), low)
        offset = offset + docs_ref[i]
    low = jnp.maximum(low, qpos - (LOOKBACK_SIZE - 1))

    def rows(r):
        return pl.ds(pl.multiple_of(r * tok, tok), tok)

    def stage_probs(h):
        x = 2 * h

        def score(r, top):
            s = lax.dot_general(win[x, r], q2[h], CONTRACT_LAST, preferred_element_type=F32) * scale
            kpos = (d - r) * tok + lax.broadcasted_iota(jnp.int32, (tok, 1), 0)
            s = jnp.where((kpos <= qpos) & (kpos >= low), s, -1e30)
            s_ref[rows(r), :] = s
            return jnp.maximum(top, jnp.max(s, axis=0, keepdims=True))

        top = lax.fori_loop(0, slots, score, jnp.full((1, cols), -1e30, F32))

        def expo(r, total):
            e = jnp.exp(s_ref[rows(r), :] - top)
            s_ref[rows(r), :] = e
            return total + jnp.sum(e, axis=0, keepdims=True)

        total = lax.fori_loop(0, slots, expo, jnp.zeros((1, cols), F32))
        inv = 1.0 / total

        def norm(r, carry):
            prob = s_ref[rows(r), :] * inv
            s_ref[rows(r), :] = prob
            p_ref[rows(r), :] = prob.astype(BF16)
            return carry

        lax.fori_loop(0, slots, norm, 0)

    def part_sums(x, lhs, rhs):
        order = list(range(slots - 2, 0, -2)) + list(range(slots - 1, -1, -2))
        for r in order:
            part = jnp.dot(lhs[r * tok : (r + 1) * tok, :], rhs, preferred_element_type=F32)
            if r % 2:
                send_odd(x, r // 2, part)
            else:
                acc[x, r // 2] = part

    def stage_scores(h):
        x = 2 * h

        def dprob(r, delta):
            dp = lax.dot_general(win[x + 1, r], g2[h], CONTRACT_LAST, preferred_element_type=F32)
            dp_ref[rows(r), :] = dp
            return delta + jnp.sum(dp * s_ref[rows(r), :], axis=0, keepdims=True)

        delta = lax.fori_loop(0, slots, dprob, jnp.zeros((1, cols), F32))

        def dscore(r, carry):
            ds = s_ref[rows(r), :] * (dp_ref[rows(r), :] - delta) * scale
            d_ref = dp_ref
            d_ref[rows(r), :] = ds
            return carry

        lax.fori_loop(0, slots, dscore, 0)

    def emit(ref, h, weights, source):
        whole = source.reshape(slots * tok, HEAD_DIM)
        res = lax.dot_general(weights, whole, CONTRACT_FIRST, preferred_element_type=F32)
        for e in range(group):
            lo = (h * group + e) * HEAD_DIM
            ref[:, lo : lo + HEAD_DIM] = res[e * tok : (e + 1) * tok, :].astype(BF16)

    for h in range(kv):
        lo = h * HEAD_DIM
        x = 2 * h
        for t in range(1, hops + 1):
            arrive(x, t)
            arrive(x + 1, t)
            if t == 1 and h + 1 < kv:
                start_own(x + 2)
                start_own(x + 3)
        arrive_sib(x)
        stage_probs(h)
        part_sums(x + 1, p_ref, g2[h])
        arrive_sib(x + 1)
        chain_step(x + 1, hops, dv_ref, lo)
        stage_scores(h)
        emit(o_ref, h, p_ref[...], win[x + 1])
        p_ref[...] = dp_ref[...].astype(BF16)
        part_sums(x, p_ref, q2[h])
        chain_step(x, hops, dk_ref, lo)
        emit(dq_ref, h, p_ref[...], win[x])
        for t in range(hops - 1, -1, -1):
            chain_step(x + 1, t, dv_ref, lo)
            chain_step(x, t, dk_ref, lo)
    for x in range(2 * kv):
        finish_sends(x)


def body(n, doc_lengths, queries, keys, values, out_grad):
    tok, width = keys.shape[1:]
    kv = width // HEAD_DIM
    cols = queries.shape[2] // width * tok
    reach = -(-min(LOOKBACK_SIZE, tok * n // 2) // tok)
    hops = -(-reach // 2)
    slots = 2 * hops + 1
    spec = pl.BlockSpec(memory_space=pltpu.VMEM)
    tile = (tok, HEAD_DIM)
    chunks = 2 * kv
    dma = pltpu.SemaphoreType.DMA((chunks, hops))
    out = pl.pallas_call(
        functools.partial(kernel, n, hops),
        out_shape=(
            jax.ShapeDtypeStruct(queries.shape[1:], BF16),
            jax.ShapeDtypeStruct(queries.shape[1:], BF16),
            jax.ShapeDtypeStruct(keys.shape[1:], BF16),
            jax.ShapeDtypeStruct(keys.shape[1:], BF16),
        ),
        in_specs=[pl.BlockSpec(memory_space=pltpu.SMEM)] + [spec] * 4,
        out_specs=(spec,) * 4,
        scratch_shapes=[
            pltpu.VMEM((chunks, slots) + tile, BF16),
            pltpu.VMEM((kv, cols, HEAD_DIM), BF16),
            pltpu.VMEM((kv, cols, HEAD_DIM), BF16),
            pltpu.VMEM((slots * tok, cols), F32),
            pltpu.VMEM((slots * tok, cols), BF16),
            pltpu.VMEM((slots * tok, cols), F32),
            pltpu.VMEM((chunks, hops + 1) + tile, F32),
            pltpu.VMEM((chunks, hops) + tile, BF16),
            pltpu.VMEM((chunks, hops) + tile, BF16),
            pltpu.VMEM((chunks, hops) + tile, BF16),
            pltpu.VMEM((chunks, hops) + tile, BF16),
        ]
        + [dma] * 8,
        compiler_params=pltpu.CompilerParams(
            collective_id=0, has_side_effects=True, vmem_limit_bytes=50 * 1024 * 1024
        ),
    )(doc_lengths, queries[0], keys[0], values[0], out_grad[0])
    return tuple(o[None] for o in out)


def solution(mesh):
    spec = P("section", ("groups", "ctx"), "tp")
    return jax.shard_map(
        functools.partial(body, mesh.shape["ctx"]),
        mesh=mesh,
        in_specs=(P("groups"),) + (spec,) * 4,
        out_specs=(spec,) * 4,
        check_vma=False,
    )
```

```python
import functools

import jax
import jax.numpy as jnp
from jax import lax
from jax.experimental import pallas as pl
from jax.experimental.pallas import tpu as pltpu
from jax.sharding import PartitionSpec as P

HEAD_DIM = 256
LOOKBACK_SIZE = 2048
F32 = jnp.float32
BF16 = jnp.bfloat16
CONTRACT_LAST = (((1,), (1,)), ((), ()))
CONTRACT_FIRST = (((0,), (0,)), ((), ()))


def kernel(
    n, hops, docs_ref, q_ref, k_ref, v_ref, g_ref, o_ref, dq_ref, dk_ref, dv_ref,
    win, q2, g2, s_ref, p_ref, dp_ref, ds_ref, acc, sbuf, cbuf, rsib, rchain,
    lk, lq, lg, fs, fr, ss, sr, bs, br, cs, cr,
):
    tok = q_ref.shape[0]
    kv = k_ref.shape[1] // HEAD_DIM
    group = q_ref.shape[1] // k_ref.shape[1]
    cols = group * tok
    slots = 2 * hops + 1
    scale = HEAD_DIM ** (-0.5)
    d = lax.axis_index("ctx")
    c = lax.rem(d, 2)
    up = lax.rem(d + 2, n)
    down = lax.rem(d + n - 2, n)
    sibling = d + 1 - 2 * c

    def remote(src, dst, send, recv, device):
        return pltpu.make_async_remote_copy(
            src_ref=src, dst_ref=dst, send_sem=send, recv_sem=recv,
            device_id={"ctx": device}, device_id_type=pl.DeviceIdType.MESH,
        )

    def fwd(x, t):
        return remote(win.at[x, 2 * t - 2], win.at[x, 2 * t], fs.at[x, t - 1], fr.at[x, t - 1], up)

    def sib(x, u):
        return remote(win.at[x, 2 * u + 2 * c], win.at[x, 2 * u + 1], ss.at[x, u], sr.at[x, u], sibling)

    def bsib(x, u):
        return remote(sbuf.at[x, u], rsib.at[x, u], bs.at[x, u], br.at[x, u], sibling)

    def chain(x, t):
        return remote(cbuf.at[x, t - 1], rchain.at[x, t - 1], cs.at[x, t - 1], cr.at[x, t - 1], down)

    def load(x):
        lo = x // 2 * HEAD_DIM
        source = v_ref if x % 2 else k_ref
        return pltpu.make_async_copy(source.at[:, lo : lo + HEAD_DIM], win.at[x, 0], lk.at[x])

    def load_rows(source, target, sem, h, e):
        lo = (h * group + e) * HEAD_DIM
        return pltpu.make_async_copy(
            source.at[:, lo : lo + HEAD_DIM], target.at[h, e * tok : (e + 1) * tok, :], sem.at[h, e]
        )

    def start_own(x):
        load(x).wait()

        @pl.when(d + 2 < n)
        def _():
            fwd(x, 1).start()

        @pl.when(c == 0)
        def _():
            sib(x, 0).start()

    def arrive(x, t):
        @pl.when(d >= 2 * t)
        def _():
            fwd(x, t).wait_recv()
            if t < hops:
                @pl.when(d + 2 < n)
                def _():
                    fwd(x, t + 1).start()

                @pl.when(c == 0)
                def _():
                    sib(x, t).start()

            @pl.when(c == 1)
            def _():
                sib(x, t - 1).start()

    def arrive_sib(x):
        for u in range(hops):
            @pl.when(d >= 2 * u + 1)
            def _():
                sib(x, u).wait_recv()

    def send_odd(x, u, part):
        sbuf[x, u] = part.astype(BF16)

        @pl.when(d >= 2 * u + 1)
        def _():
            bsib(x, u).start()

    def chain_step(x, t, out_ref, lo):
        @pl.when(d >= 2 * t)
        def _():
            if t < hops:
                @pl.when(c == 0)
                def _():
                    bsib(x, t).wait_recv()
                    acc[x, t] += rsib[x, t].astype(F32)
            if t >= 1:
                @pl.when(c == 1)
                def _():
                    bsib(x, t - 1).wait_recv()
                    acc[x, t] += rsib[x, t - 1].astype(F32)
            if t < hops:
                @pl.when(d + 2 < n)
                def _():
                    chain(x, t + 1).wait_recv()
                    acc[x, t] += rchain[x, t].astype(F32)
            if t > 0:
                cbuf[x, t - 1] = acc[x, t].astype(BF16)
                chain(x, t).start()
            else:
                out_ref[:, lo : lo + HEAD_DIM] = acc[x, t].astype(BF16)

    def finish_sends(x):
        for t in range(1, hops + 1):
            @pl.when((d + 2 < n) & (d >= 2 * t - 2))
            def _():
                fwd(x, t).wait_send()

            @pl.when(d >= 2 * t)
            def _():
                chain(x, t).wait_send()
        for u in range(hops):
            @pl.when(d >= 2 * u + 2 * c)
            def _():
                sib(x, u).wait_send()

            @pl.when(d >= 2 * u + 1)
            def _():
                bsib(x, u).wait_send()

    barrier = pltpu.get_barrier_semaphore()
    for other in (up, down, sibling):
        pl.semaphore_signal(
            barrier, inc=1, device_id={"ctx": other}, device_id_type=pl.DeviceIdType.MESH
        )
    for h in range(kv):
        load(2 * h).start()
        for e in range(group):
            load_rows(q_ref, q2, lq, h, e).start()
        load(2 * h + 1).start()
        for e in range(group):
            load_rows(g_ref, g2, lg, h, e).start()
    pl.semaphore_wait(barrier, 3)
    start_own(0)

    for h in range(kv):
        for e in range(group):
            load_rows(q_ref, q2, lq, h, e).wait()
            load_rows(g_ref, g2, lg, h, e).wait()
        q2[h] = q2[h] * BF16(scale)
    for r in range(1, slots):
        @pl.when(d < r)
        def _():
            for x in range(2 * kv):
                win[x, r] = jnp.zeros((tok, HEAD_DIM), BF16)

    qpos = d * tok + lax.rem(lax.broadcasted_iota(jnp.int32, (1, cols), 1), tok)
    low = jnp.zeros((1, cols), jnp.int32)
    offset = jnp.int32(0)
    for i in range(docs_ref.shape[0]):
        low = jnp.where(offset <= qpos, jnp.maximum(low, offset), low)
        offset = offset + docs_ref[i]
    low = jnp.maximum(low, qpos - (LOOKBACK_SIZE - 1))

    def rows(r):
        return pl.ds(r * tok, tok)

    def score(h, r, top):
        s = lax.dot_general(win[2 * h, r], q2[h], CONTRACT_LAST, preferred_element_type=F32)
        kpos = (d - r) * tok + lax.broadcasted_iota(jnp.int32, (tok, 1), 0)
        allowed = kpos >= low
        if r == 0:
            allowed = allowed & (kpos <= qpos)
        s = jnp.where(allowed, s, -1e30)
        s_ref[rows(r), :] = s
        return jnp.maximum(top, jnp.max(s, axis=0, keepdims=True))

    def probs(top):
        total = jnp.zeros((1, cols), F32)
        for r in range(slots):
            e = jnp.exp(s_ref[rows(r), :] - top)
            s_ref[rows(r), :] = e
            total = total + jnp.sum(e, axis=0, keepdims=True)
        inv = 1.0 / total
        for r in range(slots):
            prob = s_ref[rows(r), :] * inv
            s_ref[rows(r), :] = prob
            p_ref[rows(r), :] = prob.astype(BF16)

    def part_sums(x, lhs, rhs):
        order = list(range(slots - 2, 0, -2)) + list(range(slots - 1, -1, -2))
        for r in order:
            part = jnp.dot(lhs[rows(r), :], rhs, preferred_element_type=F32)
            if r % 2:
                send_odd(x, r // 2, part)
            else:
                acc[x, r // 2] = part

    def dscores(h):
        delta = jnp.zeros((1, cols), F32)
        for r in range(slots):
            dp = lax.dot_general(win[2 * h + 1, r], g2[h], CONTRACT_LAST, preferred_element_type=F32)
            dp_ref[rows(r), :] = dp
            delta = delta + jnp.sum(dp * s_ref[rows(r), :], axis=0, keepdims=True)
        for r in range(slots):
            ds_ref[rows(r), :] = (s_ref[rows(r), :] * (dp_ref[rows(r), :] - delta)).astype(BF16)

    def emit(ref, h, weights, source, factor):
        whole = source.reshape(slots * tok, HEAD_DIM)
        res = lax.dot_general(weights, whole, CONTRACT_FIRST, preferred_element_type=F32)
        if factor is not None:
            res = res * factor
        for e in range(group):
            lo = (h * group + e) * HEAD_DIM
            ref[:, lo : lo + HEAD_DIM] = res[e * tok : (e + 1) * tok, :].astype(BF16)

    for h in range(kv):
        lo = h * HEAD_DIM
        x = 2 * h
        more = h + 1 < kv
        top = score(h, 0, jnp.full((1, cols), -1e30, F32))
        if h == 0:
            arrive(x, 1)
            start_own(x + 1)
        for t in range(2, hops + 1):
            arrive(x, t)
        if h == 0:
            arrive(x + 1, 1)
            if more:
                start_own(x + 2)
        if h > 0:
            for t in range(hops - 1, 0, -1):
                chain_step(x - 2, t, dk_ref, lo - HEAD_DIM)
        arrive_sib(x)
        for r in range(1, slots):
            top = score(h, r, top)
        probs(top)
        part_sums(x + 1, p_ref, g2[h])
        chain_step(x + 1, hops, dv_ref, lo)
        if more:
            arrive(x + 2, 1)
            start_own(x + 3)
        if h > 0:
            chain_step(x - 2, 0, dk_ref, lo - HEAD_DIM)
        for t in range(2, hops + 1):
            arrive(x + 1, t)
        arrive_sib(x + 1)
        for t in range(hops - 1, 0, -1):
            chain_step(x + 1, t, dv_ref, lo)
        dscores(h)
        part_sums(x, ds_ref, q2[h])
        chain_step(x, hops, dk_ref, lo)
        chain_step(x + 1, 0, dv_ref, lo)
        if more:
            arrive(x + 3, 1)
        emit(o_ref, h, p_ref[...], win[x + 1], None)
        emit(dq_ref, h, ds_ref[...], win[x], scale)
    for t in range(hops - 1, -1, -1):
        chain_step(2 * kv - 2, t, dk_ref, (kv - 1) * HEAD_DIM)
    for x in range(2 * kv):
        finish_sends(x)


def body(n, doc_lengths, queries, keys, values, out_grad):
    tok, width = keys.shape[1:]
    kv = width // HEAD_DIM
    cols = queries.shape[2] // width * tok
    reach = -(-min(LOOKBACK_SIZE, tok * n // 2) // tok)
    hops = -(-reach // 2)
    slots = 2 * hops + 1
    spec = pl.BlockSpec(memory_space=pltpu.VMEM)
    tile = (tok, HEAD_DIM)
    chunks = 2 * kv
    dma = pltpu.SemaphoreType.DMA((chunks, hops))
    out = pl.pallas_call(
        functools.partial(kernel, n, hops),
        out_shape=(
            jax.ShapeDtypeStruct(queries.shape[1:], BF16),
            jax.ShapeDtypeStruct(queries.shape[1:], BF16),
            jax.ShapeDtypeStruct(keys.shape[1:], BF16),
            jax.ShapeDtypeStruct(keys.shape[1:], BF16),
        ),
        in_specs=[pl.BlockSpec(memory_space=pltpu.SMEM)] + [pl.BlockSpec(memory_space=pl.ANY)] * 4,
        out_specs=(spec,) * 4,
        scratch_shapes=[
            pltpu.VMEM((chunks, slots) + tile, BF16),
            pltpu.VMEM((kv, cols, HEAD_DIM), BF16),
            pltpu.VMEM((kv, cols, HEAD_DIM), BF16),
            pltpu.VMEM((slots * tok, cols), F32),
            pltpu.VMEM((slots * tok, cols), BF16),
            pltpu.VMEM((slots * tok, cols), F32),
            pltpu.VMEM((slots * tok, cols), BF16),
            pltpu.VMEM((chunks, hops + 1) + tile, F32),
            pltpu.VMEM((chunks, hops) + tile, BF16),
            pltpu.VMEM((chunks, hops) + tile, BF16),
            pltpu.VMEM((chunks, hops) + tile, BF16),
            pltpu.VMEM((chunks, hops) + tile, BF16),
        ]
        + [
            pltpu.SemaphoreType.DMA((chunks,)),
            pltpu.SemaphoreType.DMA((kv, cols // tok)),
            pltpu.SemaphoreType.DMA((kv, cols // tok)),
        ]
        + [dma] * 8,
        compiler_params=pltpu.CompilerParams(
            collective_id=0, has_side_effects=True, vmem_limit_bytes=50 * 1024 * 1024
        ),
    )(doc_lengths, queries[0], keys[0], values[0], out_grad[0])
    return tuple(o[None] for o in out)


def solution(mesh):
    spec = P("section", ("groups", "ctx"), "tp")
    return jax.shard_map(
        functools.partial(body, mesh.shape["ctx"]),
        mesh=mesh,
        in_specs=(P("groups"),) + (spec,) * 4,
        out_specs=(spec,) * 4,
        check_vma=False,
    )
```

```python
import functools

import jax
import jax.numpy as jnp
from jax import lax
from jax.experimental import pallas as pl
from jax.experimental.pallas import tpu as pltpu
from jax.sharding import PartitionSpec as P

HEAD_DIM = 256
LOOKBACK_SIZE = 2048
F32 = jnp.float32
BF16 = jnp.bfloat16
CONTRACT_LAST = (((1,), (1,)), ((), ()))
CONTRACT_FIRST = (((0,), (0,)), ((), ()))


def kernel(
    n, hops, docs_ref, q_ref, k_ref, v_ref, g_ref, o_ref, dq_ref, dk_ref, dv_ref,
    win, q2, g2, s_ref, p_ref, dp_ref, ds_ref, acc, sbuf, cbuf, rsib, rchain,
    lk, lq, lg, fs, fr, ss, sr, bs, br, cs, cr,
):
    tok = q_ref.shape[0]
    kv = k_ref.shape[1] // HEAD_DIM
    group = q_ref.shape[1] // k_ref.shape[1]
    cols = group * tok
    slots = 2 * hops + 1
    scale = HEAD_DIM ** (-0.5)
    d = lax.axis_index("ctx")
    c = lax.rem(d, 2)
    up = lax.rem(d + 2, n)
    down = lax.rem(d + n - 2, n)
    sibling = d + 1 - 2 * c

    def remote(src, dst, send, recv, device):
        return pltpu.make_async_remote_copy(
            src_ref=src, dst_ref=dst, send_sem=send, recv_sem=recv,
            device_id={"ctx": device}, device_id_type=pl.DeviceIdType.MESH,
        )

    def fwd(x, t):
        return remote(win.at[x, 2 * t - 2], win.at[x, 2 * t], fs.at[x, t - 1], fr.at[x, t - 1], up)

    def sib(x, u):
        return remote(win.at[x, 2 * u + 2 * c], win.at[x, 2 * u + 1], ss.at[x, u], sr.at[x, u], sibling)

    def bsib(x, u):
        return remote(sbuf.at[x, u], rsib.at[x, u], bs.at[x, u], br.at[x, u], sibling)

    def chain(x, t):
        return remote(cbuf.at[x, t - 1], rchain.at[x, t - 1], cs.at[x, t - 1], cr.at[x, t - 1], down)

    def load(x):
        lo = x // 2 * HEAD_DIM
        source = v_ref if x % 2 else k_ref
        return pltpu.make_async_copy(source.at[:, lo : lo + HEAD_DIM], win.at[x, 0], lk.at[x])

    def load_rows(source, target, sem, h, e):
        lo = (h * group + e) * HEAD_DIM
        return pltpu.make_async_copy(
            source.at[:, lo : lo + HEAD_DIM], target.at[h, e * tok : (e + 1) * tok, :], sem.at[h, e]
        )

    def start_own(x):
        load(x).wait()

        @pl.when(d + 2 < n)
        def _():
            fwd(x, 1).start()

        @pl.when(c == 0)
        def _():
            sib(x, 0).start()

    def arrive(x, t):
        @pl.when(d >= 2 * t)
        def _():
            fwd(x, t).wait_recv()
            if t < hops:
                @pl.when(d + 2 < n)
                def _():
                    fwd(x, t + 1).start()

                @pl.when(c == 0)
                def _():
                    sib(x, t).start()

            @pl.when(c == 1)
            def _():
                sib(x, t - 1).start()

    def arrive_sib(x):
        for u in range(hops):
            @pl.when(d >= 2 * u + 1)
            def _():
                sib(x, u).wait_recv()

    def send_odd(x, u, part):
        sbuf[x, u] = part.astype(BF16)

        @pl.when(d >= 2 * u + 1)
        def _():
            bsib(x, u).start()

    def chain_step(x, t, out_ref, lo):
        @pl.when(d >= 2 * t)
        def _():
            if t < hops:
                @pl.when(c == 0)
                def _():
                    bsib(x, t).wait_recv()
                    acc[x, t] += rsib[x, t].astype(F32)
            if t >= 1:
                @pl.when(c == 1)
                def _():
                    bsib(x, t - 1).wait_recv()
                    acc[x, t] += rsib[x, t - 1].astype(F32)
            if t < hops:
                @pl.when(d + 2 < n)
                def _():
                    chain(x, t + 1).wait_recv()
                    acc[x, t] += rchain[x, t].astype(F32)
            if t > 0:
                cbuf[x, t - 1] = acc[x, t].astype(BF16)
                chain(x, t).start()
            else:
                out_ref[:, lo : lo + HEAD_DIM] = acc[x, t].astype(BF16)

    def finish_sends(x):
        for t in range(1, hops + 1):
            @pl.when((d + 2 < n) & (d >= 2 * t - 2))
            def _():
                fwd(x, t).wait_send()

            @pl.when(d >= 2 * t)
            def _():
                chain(x, t).wait_send()
        for u in range(hops):
            @pl.when(d >= 2 * u + 2 * c)
            def _():
                sib(x, u).wait_send()

            @pl.when(d >= 2 * u + 1)
            def _():
                bsib(x, u).wait_send()

    barrier = pltpu.get_barrier_semaphore()
    for other in (up, down, sibling):
        pl.semaphore_signal(
            barrier, inc=1, device_id={"ctx": other}, device_id_type=pl.DeviceIdType.MESH
        )
    for h in range(kv):
        load(2 * h).start()
        for e in range(group):
            load_rows(q_ref, q2, lq, h, e).start()
        load(2 * h + 1).start()
        for e in range(group):
            load_rows(g_ref, g2, lg, h, e).start()
    pl.semaphore_wait(barrier, 3)
    start_own(0)
    start_own(1)

    for h in range(kv):
        for e in range(group):
            load_rows(q_ref, q2, lq, h, e).wait()
            load_rows(g_ref, g2, lg, h, e).wait()
        q2[h] = q2[h] * BF16(scale)
    for r in range(1, slots):
        @pl.when(d < r)
        def _():
            for x in range(2 * kv):
                win[x, r] = jnp.zeros((tok, HEAD_DIM), BF16)

    qpos = d * tok + lax.rem(lax.broadcasted_iota(jnp.int32, (1, cols), 1), tok)
    low = jnp.zeros((1, cols), jnp.int32)
    offset = jnp.int32(0)
    for i in range(docs_ref.shape[0]):
        low = jnp.where(offset <= qpos, jnp.maximum(low, offset), low)
        offset = offset + docs_ref[i]
    low = jnp.maximum(low, qpos - (LOOKBACK_SIZE - 1))

    def rows(r):
        return pl.ds(r * tok, tok)

    def score(h, r, top):
        s = lax.dot_general(win[2 * h, r], q2[h], CONTRACT_LAST, preferred_element_type=F32)
        kpos = (d - r) * tok + lax.broadcasted_iota(jnp.int32, (tok, 1), 0)
        allowed = kpos >= low
        if r == 0:
            allowed = allowed & (kpos <= qpos)
        s = jnp.where(allowed, s, -1e30)
        s_ref[rows(r), :] = s
        return jnp.maximum(top, jnp.max(s, axis=0, keepdims=True))

    def probs(top):
        total = jnp.zeros((1, cols), F32)
        for r in range(slots):
            e = jnp.exp(s_ref[rows(r), :] - top)
            s_ref[rows(r), :] = e
            total = total + jnp.sum(e, axis=0, keepdims=True)
        return 1.0 / total

    def normalise(h, r, inv):
        prob = s_ref[rows(r), :] * inv
        s_ref[rows(r), :] = prob
        p_ref[h, rows(r), :] = prob.astype(BF16)

    def part_sums(x, make, lhs, rhs, out_ref, lo):
        far = [slots - 2, slots - 1]
        rest = list(range(slots - 4, 0, -2)) + list(range(slots - 3, -1, -2))
        for r in far + rest:
            make(r)
            part = jnp.dot(lhs[x // 2, rows(r), :], rhs, preferred_element_type=F32)
            if r % 2:
                send_odd(x, r // 2, part)
            else:
                acc[x, r // 2] = part
            if r == slots - 1:
                chain_step(x, hops, out_ref, lo)

    def deltas(h):
        delta = jnp.zeros((1, cols), F32)
        for r in range(slots):
            dp = lax.dot_general(win[2 * h + 1, r], g2[h], CONTRACT_LAST, preferred_element_type=F32)
            dp_ref[rows(r), :] = dp
            delta = delta + jnp.sum(dp * s_ref[rows(r), :], axis=0, keepdims=True)
        return delta

    def dscore(h, r, delta):
        ds_ref[h, rows(r), :] = (s_ref[rows(r), :] * (dp_ref[rows(r), :] - delta)).astype(BF16)

    def emit(ref, h, weights, source, factor):
        whole = source.reshape(slots * tok, HEAD_DIM)
        res = lax.dot_general(weights, whole, CONTRACT_FIRST, preferred_element_type=F32)
        if factor is not None:
            res = res * factor
        for e in range(group):
            lo = (h * group + e) * HEAD_DIM
            ref[:, lo : lo + HEAD_DIM] = res[e * tok : (e + 1) * tok, :].astype(BF16)

    for h in range(kv):
        lo = h * HEAD_DIM
        x = 2 * h
        more = h + 1 < kv
        top = score(h, 0, jnp.full((1, cols), -1e30, F32))
        if h == 0:
            arrive(x, 1)
            arrive(x + 1, 1)
            if more:
                start_own(x + 2)
                start_own(x + 3)
        for t in range(2, hops + 1):
            arrive(x, t)
        if h > 0:
            for t in range(hops - 1, 0, -1):
                chain_step(x - 2, t, dk_ref, lo - HEAD_DIM)
        arrive_sib(x)
        for r in range(1, slots):
            top = score(h, r, top)
        inv = probs(top)
        part_sums(x + 1, functools.partial(normalise, h, inv=inv), p_ref, g2[h], dv_ref, lo)
        if more:
            arrive(x + 2, 1)
        if h > 0:
            chain_step(x - 2, 0, dk_ref, lo - HEAD_DIM)
        for t in range(2, hops + 1):
            arrive(x + 1, t)
        arrive_sib(x + 1)
        delta = deltas(h)
        for t in range(hops - 1, 0, -1):
            chain_step(x + 1, t, dv_ref, lo)
        part_sums(x, functools.partial(dscore, h, delta=delta), ds_ref, q2[h], dk_ref, lo)
        chain_step(x + 1, 0, dv_ref, lo)
        if more:
            arrive(x + 3, 1)
    for h in range(kv):
        emit(o_ref, h, p_ref[h], win[2 * h + 1], None)
    for t in range(hops - 1, -1, -1):
        chain_step(2 * kv - 2, t, dk_ref, (kv - 1) * HEAD_DIM)
        if t == hops - 1:
            for h in range(kv):
                emit(dq_ref, h, ds_ref[h], win[2 * h], scale)
    for x in range(2 * kv):
        finish_sends(x)


def body(n, doc_lengths, queries, keys, values, out_grad):
    tok, width = keys.shape[1:]
    kv = width // HEAD_DIM
    cols = queries.shape[2] // width * tok
    reach = -(-min(LOOKBACK_SIZE, tok * n // 2) // tok)
    hops = -(-reach // 2)
    slots = 2 * hops + 1
    spec = pl.BlockSpec(memory_space=pltpu.VMEM)
    tile = (tok, HEAD_DIM)
    chunks = 2 * kv
    dma = pltpu.SemaphoreType.DMA((chunks, hops))
    out = pl.pallas_call(
        functools.partial(kernel, n, hops),
        out_shape=(
            jax.ShapeDtypeStruct(queries.shape[1:], BF16),
            jax.ShapeDtypeStruct(queries.shape[1:], BF16),
            jax.ShapeDtypeStruct(keys.shape[1:], BF16),
            jax.ShapeDtypeStruct(keys.shape[1:], BF16),
        ),
        in_specs=[pl.BlockSpec(memory_space=pltpu.SMEM)] + [pl.BlockSpec(memory_space=pl.ANY)] * 4,
        out_specs=(spec,) * 4,
        scratch_shapes=[
            pltpu.VMEM((chunks, slots) + tile, BF16),
            pltpu.VMEM((kv, cols, HEAD_DIM), BF16),
            pltpu.VMEM((kv, cols, HEAD_DIM), BF16),
            pltpu.VMEM((slots * tok, cols), F32),
            pltpu.VMEM((kv, slots * tok, cols), BF16),
            pltpu.VMEM((slots * tok, cols), F32),
            pltpu.VMEM((kv, slots * tok, cols), BF16),
            pltpu.VMEM((chunks, hops + 1) + tile, F32),
            pltpu.VMEM((chunks, hops) + tile, BF16),
            pltpu.VMEM((chunks, hops) + tile, BF16),
            pltpu.VMEM((chunks, hops) + tile, BF16),
            pltpu.VMEM((chunks, hops) + tile, BF16),
        ]
        + [
            pltpu.SemaphoreType.DMA((chunks,)),
            pltpu.SemaphoreType.DMA((kv, cols // tok)),
            pltpu.SemaphoreType.DMA((kv, cols // tok)),
        ]
        + [dma] * 8,
        compiler_params=pltpu.CompilerParams(
            collective_id=0, has_side_effects=True, vmem_limit_bytes=50 * 1024 * 1024
        ),
    )(doc_lengths, queries[0], keys[0], values[0], out_grad[0])
    return tuple(o[None] for o in out)


def solution(mesh):
    spec = P("section", ("groups", "ctx"), "tp")
    return jax.shard_map(
        functools.partial(body, mesh.shape["ctx"]),
        mesh=mesh,
        in_specs=(P("groups"),) + (spec,) * 4,
        out_specs=(spec,) * 4,
        check_vma=False,
    )
```

```python
import functools

import jax
import jax.numpy as jnp
from jax import lax
from jax.experimental import pallas as pl
from jax.experimental.pallas import tpu as pltpu
from jax.sharding import PartitionSpec as P

HEAD_DIM = 256
LOOKBACK_SIZE = 2048
F32 = jnp.float32
BF16 = jnp.bfloat16
CONTRACT_LAST = (((1,), (1,)), ((), ()))
CONTRACT_FIRST = (((0,), (0,)), ((), ()))


def kernel(
    n, hops, docs_ref, q_ref, k_ref, v_ref, g_ref, o_ref, dq_ref, dk_ref, dv_ref,
    win, q2, g2, s_ref, p_ref, dp_ref, ds_ref, acc, sbuf, cbuf, rsib, rchain,
    lk, lq, lg, fs, fr, ss, sr, bs, br, cs, cr,
):
    tok = q_ref.shape[0]
    kv = k_ref.shape[1] // HEAD_DIM
    group = q_ref.shape[1] // k_ref.shape[1]
    cols = group * tok
    slots = 2 * hops + 1
    scale = HEAD_DIM ** (-0.5)
    d = lax.axis_index("ctx")
    c = lax.rem(d, 2)
    up = lax.rem(d + 2, n)
    down = lax.rem(d + n - 2, n)
    sibling = d + 1 - 2 * c

    def remote(src, dst, send, recv, device):
        return pltpu.make_async_remote_copy(
            src_ref=src, dst_ref=dst, send_sem=send, recv_sem=recv,
            device_id={"ctx": device}, device_id_type=pl.DeviceIdType.MESH,
        )

    def fwd(x, t):
        return remote(win.at[x, 2 * t - 2], win.at[x, 2 * t], fs.at[x, t - 1], fr.at[x, t - 1], up)

    def sib(x, u):
        return remote(win.at[x, 2 * u + 2 * c], win.at[x, 2 * u + 1], ss.at[x, u], sr.at[x, u], sibling)

    def bsib(x, u):
        return remote(sbuf.at[x, u], rsib.at[x, u], bs.at[x, u], br.at[x, u], sibling)

    def chain(x, t):
        return remote(cbuf.at[x, t - 1], rchain.at[x, t - 1], cs.at[x, t - 1], cr.at[x, t - 1], down)

    def load(x):
        lo = x // 2 * HEAD_DIM
        source = v_ref if x % 2 else k_ref
        return pltpu.make_async_copy(source.at[:, lo : lo + HEAD_DIM], win.at[x, 0], lk.at[x])

    def load_rows(source, target, sem, h, e):
        lo = (h * group + e) * HEAD_DIM
        return pltpu.make_async_copy(
            source.at[:, lo : lo + HEAD_DIM], target.at[h, e * tok : (e + 1) * tok, :], sem.at[h, e]
        )

    def start_own(x):
        load(x).wait()

        @pl.when(d + 2 < n)
        def _():
            fwd(x, 1).start()

        @pl.when(c == 0)
        def _():
            sib(x, 0).start()

    def arrive(x, t):
        @pl.when(d >= 2 * t)
        def _():
            fwd(x, t).wait_recv()
            if t < hops:
                @pl.when(d + 2 < n)
                def _():
                    fwd(x, t + 1).start()

                @pl.when(c == 0)
                def _():
                    sib(x, t).start()

            @pl.when(c == 1)
            def _():
                sib(x, t - 1).start()

    def arrive_sib(x):
        for u in range(hops):
            @pl.when(d >= 2 * u + 1)
            def _():
                sib(x, u).wait_recv()

    def send_odd(x, u, part):
        sbuf[x, u] = part.astype(BF16)

        @pl.when(d >= 2 * u + 1)
        def _():
            bsib(x, u).start()

    def chain_step(x, t, out_ref, lo):
        @pl.when(d >= 2 * t)
        def _():
            if t < hops:
                @pl.when(c == 0)
                def _():
                    bsib(x, t).wait_recv()
                    acc[x, t] += rsib[x, t].astype(F32)
            if t >= 1:
                @pl.when(c == 1)
                def _():
                    bsib(x, t - 1).wait_recv()
                    acc[x, t] += rsib[x, t - 1].astype(F32)
            if t < hops:
                @pl.when(d + 2 < n)
                def _():
                    chain(x, t + 1).wait_recv()
                    acc[x, t] += rchain[x, t].astype(F32)
            if t > 0:
                cbuf[x, t - 1] = acc[x, t].astype(BF16)
                chain(x, t).start()
            else:
                out_ref[:, lo : lo + HEAD_DIM] = acc[x, t].astype(BF16)

    def finish_sends(x):
        for t in range(1, hops + 1):
            @pl.when((d + 2 < n) & (d >= 2 * t - 2))
            def _():
                fwd(x, t).wait_send()

            @pl.when(d >= 2 * t)
            def _():
                chain(x, t).wait_send()
        for u in range(hops):
            @pl.when(d >= 2 * u + 2 * c)
            def _():
                sib(x, u).wait_send()

            @pl.when(d >= 2 * u + 1)
            def _():
                bsib(x, u).wait_send()

    barrier = pltpu.get_barrier_semaphore()
    for other in (up, down, sibling):
        pl.semaphore_signal(
            barrier, inc=1, device_id={"ctx": other}, device_id_type=pl.DeviceIdType.MESH
        )
    for h in range(kv):
        load(2 * h).start()
        for e in range(group):
            load_rows(q_ref, q2, lq, h, e).start()
        load(2 * h + 1).start()
        for e in range(group):
            load_rows(g_ref, g2, lg, h, e).start()
    pl.semaphore_wait(barrier, 3)
    start_own(0)
    start_own(1)

    for h in range(kv):
        for e in range(group):
            load_rows(q_ref, q2, lq, h, e).wait()
            load_rows(g_ref, g2, lg, h, e).wait()
        q2[h] = q2[h] * BF16(scale)
    for r in range(1, slots):
        @pl.when(d < r)
        def _():
            for x in range(2 * kv):
                win[x, r] = jnp.zeros((tok, HEAD_DIM), BF16)

    qpos = d * tok + lax.rem(lax.broadcasted_iota(jnp.int32, (1, cols), 1), tok)
    low = jnp.zeros((1, cols), jnp.int32)
    offset = jnp.int32(0)
    for i in range(docs_ref.shape[0]):
        low = jnp.where(offset <= qpos, jnp.maximum(low, offset), low)
        offset = offset + docs_ref[i]
    low = jnp.maximum(low, qpos - (LOOKBACK_SIZE - 1))

    def rows(r):
        return pl.ds(r * tok, tok)

    def score(h, r, top):
        s = lax.dot_general(win[2 * h, r], q2[h], CONTRACT_LAST, preferred_element_type=F32)
        kpos = (d - r) * tok + lax.broadcasted_iota(jnp.int32, (tok, 1), 0)
        allowed = kpos >= low
        if r == 0:
            allowed = allowed & (kpos <= qpos)
        s = jnp.where(allowed, s, -1e30)
        s_ref[rows(r), :] = s
        return jnp.maximum(top, jnp.max(s, axis=0, keepdims=True))

    def probs(top):
        total = jnp.zeros((1, cols), F32)
        for r in range(slots):
            e = jnp.exp(s_ref[rows(r), :] - top)
            s_ref[rows(r), :] = e
            total = total + jnp.sum(e, axis=0, keepdims=True)
        return 1.0 / total

    def normalise(h, r, inv):
        prob = s_ref[rows(r), :] * inv
        s_ref[rows(r), :] = prob
        p_ref[h, rows(r), :] = prob.astype(BF16)

    def part_sums(x, make, lhs, rhs, out_ref, lo):
        far = [slots - 2, slots - 1]
        rest = list(range(slots - 4, 0, -2)) + list(range(slots - 3, -1, -2))
        for r in far + rest:
            make(r)
            part = jnp.dot(lhs[x // 2, rows(r), :], rhs, preferred_element_type=F32)
            if r % 2:
                send_odd(x, r // 2, part)
            else:
                acc[x, r // 2] = part
            if r == slots - 1:
                chain_step(x, hops, out_ref, lo)

    def deltas(h):
        delta = jnp.zeros((1, cols), F32)
        for r in range(slots):
            dp = lax.dot_general(win[2 * h + 1, r], g2[h], CONTRACT_LAST, preferred_element_type=F32)
            dp_ref[rows(r), :] = dp
            delta = delta + jnp.sum(dp * s_ref[rows(r), :], axis=0, keepdims=True)
        return delta

    def dscore(h, r, delta):
        ds_ref[h, rows(r), :] = (s_ref[rows(r), :] * (dp_ref[rows(r), :] - delta)).astype(BF16)

    def emit(ref, h, weights, source, factor):
        whole = source.reshape(slots * tok, HEAD_DIM)
        res = lax.dot_general(weights, whole, CONTRACT_FIRST, preferred_element_type=F32)
        if factor is not None:
            res = res * factor
        for e in range(group):
            lo = (h * group + e) * HEAD_DIM
            ref[:, lo : lo + HEAD_DIM] = res[e * tok : (e + 1) * tok, :].astype(BF16)

    for h in range(kv):
        lo = h * HEAD_DIM
        x = 2 * h
        more = h + 1 < kv
        top = score(h, 0, jnp.full((1, cols), -1e30, F32))
        if h == 0:
            arrive(x, 1)
            arrive(x + 1, 1)
            if more:
                start_own(x + 2)
                start_own(x + 3)
        for t in range(2, hops + 1):
            arrive(x, t)
        if h > 0:
            for t in range(hops - 1, 0, -1):
                chain_step(x - 2, t, dk_ref, lo - HEAD_DIM)
        arrive_sib(x)
        for r in range(1, slots):
            top = score(h, r, top)
        inv = probs(top)
        part_sums(x + 1, functools.partial(normalise, h, inv=inv), p_ref, g2[h], dv_ref, lo)
        if more:
            arrive(x + 2, 1)
        if h > 0:
            chain_step(x - 2, 0, dk_ref, lo - HEAD_DIM)
        for t in range(2, hops + 1):
            arrive(x + 1, t)
        arrive_sib(x + 1)
        delta = deltas(h)
        part_sums(x, functools.partial(dscore, h, delta=delta), ds_ref, q2[h], dk_ref, lo)
        for t in range(hops - 1, 0, -1):
            chain_step(x + 1, t, dv_ref, lo)
        chain_step(x + 1, 0, dv_ref, lo)
        if more:
            arrive(x + 3, 1)
    for h in range(kv):
        emit(o_ref, h, p_ref[h], win[2 * h + 1], None)
    for t in range(hops - 1, -1, -1):
        chain_step(2 * kv - 2, t, dk_ref, (kv - 1) * HEAD_DIM)
        if t == hops - 1:
            for h in range(kv):
                emit(dq_ref, h, ds_ref[h], win[2 * h], scale)
    for x in range(2 * kv):
        finish_sends(x)


def body(n, doc_lengths, queries, keys, values, out_grad):
    tok, width = keys.shape[1:]
    kv = width // HEAD_DIM
    cols = queries.shape[2] // width * tok
    reach = -(-min(LOOKBACK_SIZE, tok * n // 2) // tok)
    hops = -(-reach // 2)
    slots = 2 * hops + 1
    spec = pl.BlockSpec(memory_space=pltpu.VMEM)
    tile = (tok, HEAD_DIM)
    chunks = 2 * kv
    dma = pltpu.SemaphoreType.DMA((chunks, hops))
    out = pl.pallas_call(
        functools.partial(kernel, n, hops),
        out_shape=(
            jax.ShapeDtypeStruct(queries.shape[1:], BF16),
            jax.ShapeDtypeStruct(queries.shape[1:], BF16),
            jax.ShapeDtypeStruct(keys.shape[1:], BF16),
            jax.ShapeDtypeStruct(keys.shape[1:], BF16),
        ),
        in_specs=[pl.BlockSpec(memory_space=pltpu.SMEM)] + [pl.BlockSpec(memory_space=pl.ANY)] * 4,
        out_specs=(spec,) * 4,
        scratch_shapes=[
            pltpu.VMEM((chunks, slots) + tile, BF16),
            pltpu.VMEM((kv, cols, HEAD_DIM), BF16),
            pltpu.VMEM((kv, cols, HEAD_DIM), BF16),
            pltpu.VMEM((slots * tok, cols), F32),
            pltpu.VMEM((kv, slots * tok, cols), BF16),
            pltpu.VMEM((slots * tok, cols), F32),
            pltpu.VMEM((kv, slots * tok, cols), BF16),
            pltpu.VMEM((chunks, hops + 1) + tile, F32),
            pltpu.VMEM((chunks, hops) + tile, BF16),
            pltpu.VMEM((chunks, hops) + tile, BF16),
            pltpu.VMEM((chunks, hops) + tile, BF16),
            pltpu.VMEM((chunks, hops) + tile, BF16),
        ]
        + [
            pltpu.SemaphoreType.DMA((chunks,)),
            pltpu.SemaphoreType.DMA((kv, cols // tok)),
            pltpu.SemaphoreType.DMA((kv, cols // tok)),
        ]
        + [dma] * 8,
        compiler_params=pltpu.CompilerParams(
            collective_id=0, has_side_effects=True, vmem_limit_bytes=50 * 1024 * 1024
        ),
    )(doc_lengths, queries[0], keys[0], values[0], out_grad[0])
    return tuple(o[None] for o in out)


def solution(mesh):
    spec = P("section", ("groups", "ctx"), "tp")
    return jax.shard_map(
        functools.partial(body, mesh.shape["ctx"]),
        mesh=mesh,
        in_specs=(P("groups"),) + (spec,) * 4,
        out_specs=(spec,) * 4,
        check_vma=False,
    )
```
